32 devices in a mesh: region: 4 (over x, core), tile: 8 (over z, y).
Axes of the slice: x: 2, y: 2, z: 4, core: 2. Of those that a mesh axis runs over, the one named last changes fastest.
Arguments:
- quantized: bfloat16 [131072, 1024], P(('region', 'tile')), may hold values from -6 to 6
- block_scales: float32 [8, 131072], P(None, ('region', 'tile')), may hold values from 0.25 to 4
- band_width: int32 [32], replicated, may hold values from 1 to 256, as said below
- valid_count: int32 [32], P(('region', 'tile')), may hold values from 1024 to 4096, as said below
- prior_basis: float32 [1024, 64], replicated, may hold values from -0.1875 to 0.1875
Outputs:
- projected: float32 [64, 131072], P(None, ('region', 'tile'))
- new_basis: float32 [1024, 64], replicated
The draws below stay inside these ranges and needn't reach their ends.
Inputs may be any that keep to these rules, and one draw needn't show every extreme that they name: `band_width`: some tile other than the first of its region has width 256 in every draw. `valid_count`: the last tile's count is 4096 in every draw.
All inputs are finite; a program needn't handle non-finite values.
Results may differ from the reference program's by a relative error of at most 0.0016.
Values may be sent and summed in bfloat16 or wider, within the bound.
A program may use at most 128 MiB of HBM per device.

```python
import math
import jax
import jax.numpy as jnp
from jax import lax

D = 1024
K = 64
BLOCK = 128
BAND = 256
TOK_DEV = 4096
TILES = 32
TOKENS = 131072
NB = 8
N_REGION = 4
N_TILE = 8


def draw_quantized(key, part):
    noise_key, offset_key = jax.random.split(jax.random.fold_in(key, 101), 2)
    offsets = jax.random.normal(offset_key, (D,), jnp.float32) * 0.7
    ramp = 1.0 + 2.0 * jnp.arange(TOKENS, dtype=jnp.float32) / (TOKENS - 1)
    noise = jax.random.normal(noise_key, (TOKENS, D), jnp.float32)
    values = jnp.clip(noise + ramp[:, None] * offsets[None, :], -6.0, 6.0)
    return values.astype(jnp.bfloat16)


def draw_band_width(key, part):
    first_key, second_key, third_key = jax.random.split(jax.random.fold_in(key, 202), 3)
    widths = jax.random.randint(first_key, (TILES,), 1, BAND + 1)
    chosen = jax.random.randint(second_key, (), 0, N_REGION) * N_TILE + jax.random.randint(third_key, (), 1, N_TILE)
    return widths.at[chosen].set(BAND).astype(jnp.int32)


def draw_valid_count(key, part):
    jitter_key = jax.random.fold_in(key, 303)
    lowest = TOK_DEV // 3
    positions = jnp.arange(TILES, dtype=jnp.int32)
    baseline = lowest + positions * (TOK_DEV - lowest) // max(TILES - 1, 1)
    jitter = jax.random.randint(jitter_key, (TILES,), -(TOK_DEV // 8), TOK_DEV // 8 + 1)
    counts = jnp.clip(baseline + jitter, TOK_DEV // 4, TOK_DEV)
    return counts.at[TILES - 1].set(TOK_DEV).astype(jnp.int32)


def level_of(own_key, shape, cuts, least, top_value):
    gain, own = 1.0, jax.random.fold_in(own_key, 6)
    for dim, shards_of in cuts:
        heights = jnp.exp(jax.random.uniform(jax.random.fold_in(own, dim), (shards_of,), jnp.float32, least / len(cuts), top_value / len(cuts)))
        gain = gain * jnp.repeat(heights, shape[dim] // shards_of).reshape([-1 if axis == dim else 1 for axis in range(len(shape))])
    return gain


def gaussian(stream_key, dims, width, limit, held_as=jnp.bfloat16):
    array = jax.random.normal(stream_key, dims, jnp.float32) * width
    return jnp.minimum(jnp.maximum(array, -limit), limit).astype(held_as)


def setup_inputs(seed: int = 0) -> dict:
    key_of = jax.random.split(jax.random.key(seed), 6)
    quantized = draw_quantized(jax.random.fold_in(key_of[5], 71), 0)
    block_scales = jnp.clip(jnp.exp(math.log(4.0) - 2.7725887 * jax.random.uniform(key_of[1], (NB, TOKENS), jnp.float32) ** level_of(key_of[1], (NB, TOKENS), ((1, 32),), -0.2, 0.2)), 0.25, 4.0)
    band_width = draw_band_width(jax.random.fold_in(key_of[5], 71), 0)
    valid_count = draw_valid_count(jax.random.fold_in(key_of[5], 71), 0)
    prior_basis = gaussian(key_of[4], (D, K), D ** -0.5, 0.1875, jnp.float32)
    return dict(quantized=quantized, block_scales=block_scales, band_width=band_width, valid_count=valid_count, prior_basis=prior_basis)


def dequantize(quant_tile, scale_tile):
    blocks = quant_tile.astype(jnp.float32).reshape(TOK_DEV, D // BLOCK, BLOCK) * scale_tile.T[:, :, None]
    return blocks.reshape(TOK_DEV, D).astype(jnp.bfloat16)

def blend(initial, neighbour, chosen):
    summed = (initial.astype(jnp.float32) + neighbour.astype(jnp.float32)) * 0.5
    return jnp.where(chosen[:, None], summed, initial.astype(jnp.float32)).astype(jnp.bfloat16)

def reference(quantized, block_scales, band_width, valid_count, prior_basis):
    tile_count = N_REGION * N_TILE
    quant_tiles = quantized.reshape(tile_count, TOK_DEV, D)
    scale_tiles = block_scales.reshape(D // BLOCK, tile_count, TOK_DEV).transpose(1, 0, 2)
    restored = lax.map(lambda pieces: dequantize(pieces[0], pieces[1]), (quant_tiles, scale_tiles))
    position = jnp.arange(tile_count) % N_TILE
    left_width = jnp.where(position > 0, band_width, 0).astype(jnp.int32)
    right_width = jnp.where(position < N_TILE - 1, jnp.roll(band_width, -1), 0).astype(jnp.int32)
    head_rows = restored[:, :BAND]
    tail_rows = restored[:, TOK_DEV - BAND:]
    prev_tails = jnp.roll(tail_rows, 1, axis=0)
    next_heads = jnp.roll(head_rows, -1, axis=0)
    positions = jnp.arange(BAND)

    def edges(head_tile, tail_tile, prev_tail, next_head, lwidth, rwidth):
        blank = jnp.zeros((BAND, D), jnp.bfloat16)
        left_part = lax.dynamic_slice_in_dim(jnp.concatenate([prev_tail, blank], 0), (BAND - lwidth).astype(jnp.int32), BAND, 0)
        right_part = lax.dynamic_slice_in_dim(jnp.concatenate([blank, next_head], 0), rwidth.astype(jnp.int32), BAND, 0)
        return (blend(head_tile, left_part, positions < lwidth), blend(tail_tile, right_part, positions >= BAND - rwidth))
    new_heads, new_tails = jax.vmap(edges)(head_rows, tail_rows, prev_tails, next_heads, left_width, right_width)
    blended = restored.at[:, :BAND].set(new_heads).at[:, TOK_DEV - BAND:].set(new_tails)
    usable = jnp.arange(TOK_DEV)[None, :] < valid_count[:, None]
    masked = jnp.where(usable[:, :, None], blended, jnp.zeros((), jnp.bfloat16))

    def accumulate(running, tile_rows):
        products, feature_sums = running
        products = products + lax.dot_general(tile_rows.astype(jnp.float32), tile_rows.astype(jnp.float32), (((0,), (0,)), ((), ())), preferred_element_type=jnp.float32)
        feature_sums = feature_sums + jnp.sum(tile_rows.astype(jnp.float32), axis=0)
        return ((products, feature_sums), None)
    start_state = (jnp.zeros((D, D), jnp.float32), jnp.zeros((D,), jnp.float32))
    (products, feature_sums), _ = lax.scan(accumulate, start_state, masked)
    token_count = jnp.sum(valid_count.astype(jnp.float32))
    average = feature_sums / token_count
    gram = products - jnp.outer(feature_sums, average)
    update = jnp.dot(gram, prior_basis, precision=lax.Precision.HIGHEST)
    cross_sum = jnp.dot(update.T, update, precision=lax.Precision.HIGHEST)
    factor = jnp.linalg.cholesky(cross_sum)
    new_basis = jax.scipy.linalg.solve_triangular(factor, update.T, lower=True).T

    def project(pieces):
        tile_rows, usable_rows = pieces
        centred = jnp.where(usable_rows[:, None], tile_rows.astype(jnp.float32) - average, 0.0)
        return lax.dot_general(new_basis, centred, (((0,), (1,)), ((), ())), precision=lax.Precision.HIGHEST)
    projected = lax.map(project, (masked, usable))
    projected = projected.transpose(1, 0, 2).reshape(K, TOKENS)
    return (projected, new_basis)
```

```python
import functools

import jax
import jax.numpy as jnp
from jax import lax
from jax.experimental import pallas as pl
from jax.experimental.pallas import tpu as pltpu
from jax.sharding import PartitionSpec as P

BAND = 256
MESH = pl.DeviceIdType.MESH
F32 = jnp.float32
BF16 = jnp.bfloat16
HIGH = lax.Precision.HIGHEST
NT = (((1,), (1,)), ((), ()))
NN = (((1,), (0,)), ((), ()))


def split(value):
    hi = value.astype(BF16)
    lo = (value - hi.astype(F32)).astype(BF16)
    return hi, lo


def kernel(
    n_region, n_tile, owners, width,
    bw_ref, vc_ref, q_ref, sc_ref, p_ref,
    out_ref, basis_ref,
    rows, acc, parts, edge, head_msg, head_got, z_msg, z_got,
    local, extra, got, got_extra, total, total_extra,
    in_sem, m_send, m_recv, z_send, z_recv,
    rs_send, rs_recv, rx_send, rx_recv, ag_send, ag_recv, ax_send, ax_recv,
):
    tokens, feats = rows.shape
    k = p_ref.shape[1]
    count = tokens // BAND
    last = count - 1
    devices = n_region * n_tile
    region, tile = lax.axis_index("region"), lax.axis_index("tile")
    me = region * n_tile + tile
    per_row = feats // width

    def where_is(flat):
        return (lax.div(flat, n_tile), lax.rem(flat, n_tile))

    def span(c):
        return pl.ds(pl.multiple_of(c * BAND, BAND), BAND)

    def fetch(c):
        return pltpu.make_async_copy(q_ref.at[span(c)], rows.at[span(c)], in_sem.at[c])

    fetch(0).start()
    fetch(last).start()

    @pl.loop(1, last)
    def _(c):
        fetch(c).start()

    barrier = pltpu.get_barrier_semaphore()

    @pl.loop(1, devices)
    def _(d):
        pl.semaphore_signal(
            barrier, inc=1, device_id=where_is(lax.rem(me + d, devices)), device_id_type=MESH
        )

    basis_t = p_ref[...].T
    hi, lo = split(basis_t)
    parts[pl.ds(0, k), :] = hi
    parts[pl.ds(k, k), :] = lo
    acc[...] = jnp.zeros_like(acc)

    valid = vc_ref[0]
    left_width = jnp.where(tile > 0, bw_ref[me], 0)
    right_width = jnp.where(tile < n_tile - 1, bw_ref[jnp.minimum(me + 1, devices - 1)], 0)
    place = lax.broadcasted_iota(jnp.int32, (1, BAND), 1)

    def ones(cond):
        return jnp.where(cond, 1.0, 0.0).astype(F32)

    def restore(c):
        fetch(c).wait()
        scale = sc_ref[:, span(c)].T
        step = feats // scale.shape[1]
        for j in range(scale.shape[1]):
            cols = pl.ds(j * step, step)
            rows[span(c), cols] = (
                rows[span(c), cols].astype(F32) * scale[:, j : j + 1]
            ).astype(BF16)

    def project(c):
        both = lax.dot_general(parts[...], rows[span(c), :], NT, preferred_element_type=F32)
        return both[:k] + both[k:]

    def gather_update(c, weighted, weights):
        hi, lo = split(weighted)
        ones_rows = jnp.broadcast_to(weights, (16, BAND)).astype(BF16)
        lhs = jnp.concatenate([hi, lo, ones_rows], axis=0)
        acc[...] += lax.dot_general(lhs, rows[span(c), :], NN, preferred_element_type=F32)

    def to_left(src, dst, send, recv):
        return pltpu.make_async_remote_copy(
            src_ref=src.at[0], dst_ref=dst.at[1], send_sem=send.at[0], recv_sem=recv.at[1],
            device_id=(region, jnp.maximum(tile - 1, 0)), device_id_type=MESH,
        )

    def to_right(src, dst, send, recv):
        return pltpu.make_async_remote_copy(
            src_ref=src.at[1], dst_ref=dst.at[0], send_sem=send.at[1], recv_sem=recv.at[0],
            device_id=(region, jnp.minimum(tile + 1, n_tile - 1)), device_id_type=MESH,
        )

    has_left, has_right = tile > 0, tile < n_tile - 1

    def swap_start(src, dst, send, recv):
        @pl.when(has_left)
        def _():
            to_left(src, dst, send, recv).start()

        @pl.when(has_right)
        def _():
            to_right(src, dst, send, recv).start()

    def swap_wait(src, dst, send, recv):
        @pl.when(has_left)
        def _():
            to_left(src, dst, send, recv).wait_send()
            to_right(src, dst, send, recv).wait_recv()

        @pl.when(has_right)
        def _():
            to_right(src, dst, send, recv).wait_send()
            to_left(src, dst, send, recv).wait_recv()

    @pl.when(tile == 0)
    def _():
        head_got[0] = jnp.zeros(head_got.shape[1:], BF16)
        z_got[0] = jnp.zeros(z_got.shape[1:], BF16)

    @pl.when(tile == n_tile - 1)
    def _():
        head_got[1] = jnp.zeros(head_got.shape[1:], BF16)
        z_got[1] = jnp.zeros(z_got.shape[1:], BF16)

    count_hi = lax.shift_right_logical(valid, 6)
    count_lo = valid - count_hi * 64
    for side, c in ((0, 0), (1, last)):
        restore(c)
        own = project(c)
        edge[side] = own
        hi, lo = split(own)
        head_msg[side, pl.ds(0, k), :] = hi
        head_msg[side, pl.ds(k, k), :] = lo
        head_msg[side, pl.ds(2 * k, 16), :] = jnp.full((16, BAND), count_hi.astype(F32), F32).astype(BF16)
        head_msg[side, pl.ds(2 * k + 16, 16), :] = jnp.full((16, BAND), count_lo.astype(F32), F32).astype(BF16)

    pl.semaphore_wait(barrier, devices - 1)
    swap_start(head_msg, head_got, m_send, m_recv)

    @pl.loop(1, last)
    def _(c):
        restore(c)
        weights = ones(c * BAND + place < valid)
        gather_update(c, project(c) * weights, weights)

    from_row = lax.broadcasted_iota(jnp.int32, (BAND, BAND), 0)
    to_col = lax.broadcasted_iota(jnp.int32, (BAND, BAND), 1)
    shifts = (BAND - left_width, right_width - BAND)
    paired = (place < left_width, place >= BAND - right_width)
    own_valid = (ones(place < valid), ones(tokens - BAND + place < valid))

    def aligned(side, message):
        pick = ones(from_row == to_col + shifts[side]).astype(BF16)
        moved = lax.dot_general(message, pick, NN, preferred_element_type=F32)
        return moved[:k] + moved[k:]

    swap_wait(head_msg, head_got, m_send, m_recv)
    for side, c in ((0, 0), (1, last)):
        other = aligned(side, head_got[side, pl.ds(0, 2 * k), :])
        hi = head_got[side, pl.ds(2 * k, 16), :].astype(F32)
        lo = head_got[side, pl.ds(2 * k + 16, 16), :].astype(F32)
        other_count = (hi * 64.0 + lo)[:1]
        start = tokens - left_width if side == 0 else right_width - BAND
        other_valid = ones((place + start).astype(F32) < other_count)
        both = own_valid[side] + other_valid
        own = edge[side]
        weighted = jnp.where(
            paired[side], (own + other) * (both * 0.25), own * own_valid[side]
        )
        weights = jnp.where(paired[side], both * 0.5, own_valid[side])
        gather_update(c, weighted, weights)

    local[...] = acc[pl.ds(0, k), :] + acc[pl.ds(k, k), :]
    sums = acc[pl.ds(2 * k, 8), :][:1]
    groups = feats // 128
    extra[...] = jnp.concatenate(
        [
            jnp.concatenate([sums[:, i * 128 : (i + 1) * 128] for i in range(groups)], axis=0),
            jnp.full((groups, 128), valid.astype(F32), F32),
        ],
        axis=1,
    )

    def chunk(ref, i):
        return ref.at[
            pl.ds(pl.multiple_of(lax.div(i, per_row) * 8, 8), 8),
            pl.ds(pl.multiple_of(lax.rem(i, per_row) * width, 128), width),
        ]

    def scatter(d):
        target = lax.rem(me + d, devices)
        return pltpu.make_async_remote_copy(
            src_ref=chunk(local, lax.rem(target, owners)), dst_ref=got.at[d - 1],
            send_sem=rs_send.at[d - 1], recv_sem=rs_recv.at[d - 1],
            device_id=where_is(target), device_id_type=MESH,
        )

    def scatter_extra(d):
        return pltpu.make_async_remote_copy(
            src_ref=extra, dst_ref=got_extra.at[d - 1],
            send_sem=rx_send, recv_sem=rx_recv.at[d - 1],
            device_id=where_is(lax.rem(me + d, devices)), device_id_type=MESH,
        )

    def spread(d):
        mine = chunk(total, lax.rem(me, owners))
        return pltpu.make_async_remote_copy(
            src_ref=mine, dst_ref=mine,
            send_sem=ag_send.at[d - 1], recv_sem=ag_recv.at[d - 1],
            device_id=where_is(lax.rem(me + d, devices)), device_id_type=MESH,
        )

    def spread_extra(d):
        return pltpu.make_async_remote_copy(
            src_ref=total_extra, dst_ref=total_extra,
            send_sem=ax_send.at[d - 1], recv_sem=ax_recv,
            device_id=where_is(lax.rem(me + d, devices)), device_id_type=MESH,
        )

    @pl.when(me != 0)
    def _():
        scatter_extra(devices - me).start()

    @pl.loop(1, devices)
    def _(d):
        @pl.when(lax.rem(me + d, devices) < owners)
        def _():
            scatter(d).start()

    @pl.when(me == 0)
    def _():
        @pl.loop(1, devices)
        def _(d):
            scatter_extra(d).wait_recv()

        def add(d, so_far):
            return so_far + got_extra[d]

        total_extra[...] = lax.fori_loop(0, devices - 1, add, extra[...])

        @pl.loop(1, devices)
        def _(d):
            spread_extra(d).start()

    @pl.when(me < owners)
    def _():
        @pl.loop(1, devices)
        def _(d):
            scatter(d).wait_recv()

        def add(d, so_far):
            return so_far + got[d]

        chunk(total, lax.rem(me, owners))[...] = lax.fori_loop(
            0, devices - 1, add, chunk(local, lax.rem(me, owners))[...]
        )

        @pl.loop(1, devices)
        def _(d):
            spread(d).start()

    @pl.when(me != 0)
    def _():
        spread_extra(1).wait_recv()

    @pl.loop(1, devices)
    def _(d):
        @pl.when(lax.rem(me + devices - d, devices) < owners)
        def _():
            spread(d).wait_recv()

    packed = total_extra[...]
    token_count = packed[:1, 128:129]
    sums = jnp.concatenate([packed[i : i + 1, :128] for i in range(groups)], axis=1)
    average = sums / token_count
    mean_image = jnp.sum(p_ref[...].T * average, axis=1, keepdims=True)
    update = total[...] - mean_image * sums
    cross = lax.dot_general(update, update, NT, precision=HIGH, preferred_element_type=F32)
    row = lax.broadcasted_iota(jnp.int32, (k, k), 0)
    col = lax.broadcasted_iota(jnp.int32, (k, k), 1)
    work = jnp.concatenate([cross, ones(row == col)], axis=1)
    line = lax.broadcasted_iota(jnp.int32, (k, 1), 0)
    for i in range(k - 1):
        pivot = work[i : i + 1, :]
        scaled = pivot * (1.0 / pivot[:, i : i + 1])
        work = work - jnp.where(line > i, work[:, i : i + 1], 0.0) * scaled
    diagonal = jnp.sum(jnp.where(row == col, work[:, :k], 0.0), axis=1, keepdims=True)
    inverse = work[:, k:] / jnp.sqrt(diagonal)
    new_t = lax.dot_general(inverse, update, NN, precision=HIGH, preferred_element_type=F32)
    basis_ref[...] = new_t.T
    shift = jnp.sum(new_t * average, axis=1, keepdims=True)
    hi, lo = split(new_t)
    parts[pl.ds(0, k), :] = hi
    parts[pl.ds(k, k), :] = lo

    for side, c in ((0, 0), (1, last)):
        own = project(c)
        edge[side] = own
        hi, lo = split(own)
        z_msg[side, pl.ds(0, k), :] = hi
        z_msg[side, pl.ds(k, k), :] = lo
    swap_start(z_msg, z_got, z_send, z_recv)

    @pl.loop(1, last)
    def _(c):
        usable = c * BAND + place < valid
        out_ref[:, span(c)] = jnp.where(usable, project(c) - shift, 0.0)

    swap_wait(z_msg, z_got, z_send, z_recv)
    for side, c in ((0, 0), (1, last)):
        other = aligned(side, z_got[side])
        own = edge[side]
        mixed = jnp.where(paired[side], (own + other) * 0.5, own)
        out_ref[:, span(c)] = jnp.where(own_valid[side] > 0.5, mixed - shift, 0.0)

    @pl.when(me != 0)
    def _():
        scatter_extra(devices - me).wait_send()

    @pl.when(me == 0)
    def _():
        @pl.loop(1, devices)
        def _(d):
            spread_extra(d).wait_send()

    @pl.when(me < owners)
    def _():
        @pl.loop(1, devices)
        def _(d):
            spread(d).wait_send()

    @pl.loop(1, devices)
    def _(d):
        @pl.when(lax.rem(me + d, devices) < owners)
        def _():
            scatter(d).wait_send()


def per_device(n_region, n_tile, quantized, block_scales, band_width, valid_count, prior_basis):
    tokens, feats = quantized.shape
    k = prior_basis.shape[1]
    devices = n_region * n_tile
    tiles = (k // 8) * (feats // 128)
    owners = min(devices, tiles)
    width = 128 * (tiles // owners)
    others = devices - 1
    dma = pltpu.SemaphoreType.DMA
    vmem = pl.BlockSpec(memory_space=pltpu.VMEM)
    smem = pl.BlockSpec(memory_space=pltpu.SMEM)
    return pl.pallas_call(
        functools.partial(kernel, n_region, n_tile, owners, width),
        out_shape=(
            jax.ShapeDtypeStruct((k, tokens), F32),
            jax.ShapeDtypeStruct((feats, k), F32),
        ),
        in_specs=[smem, smem, pl.BlockSpec(memory_space=pl.ANY), vmem, vmem],
        out_specs=(vmem, vmem),
        scratch_shapes=[
            pltpu.VMEM((tokens, feats), BF16),
            pltpu.VMEM((2 * k + 16, feats), F32),
            pltpu.VMEM((2 * k, feats), BF16),
            pltpu.VMEM((2, k, BAND), F32),
            pltpu.VMEM((2, 2 * k + 32, BAND), BF16),
            pltpu.VMEM((2, 2 * k + 32, BAND), BF16),
            pltpu.VMEM((2, 2 * k, BAND), BF16),
            pltpu.VMEM((2, 2 * k, BAND), BF16),
            pltpu.VMEM((k, feats), F32),
            pltpu.VMEM((feats // 128, 256), F32),
            pltpu.VMEM((others, 8, width), F32),
            pltpu.VMEM((others, feats // 128, 256), F32),
            pltpu.VMEM((k, feats), F32),
            pltpu.VMEM((feats // 128, 256), F32),
            dma((tokens // BAND,)),
            dma((2,)), dma((2,)), dma((2,)), dma((2,)),
            dma((others,)), dma((others,)), dma(()), dma((others,)),
            dma((others,)), dma((others,)), dma((others,)), dma(()),
        ],
        compiler_params=pltpu.CompilerParams(
            collective_id=0, has_side_effects=True, vmem_limit_bytes=48 * 1024 * 1024
        ),
    )(band_width, valid_count, quantized, block_scales, prior_basis)


def solution(mesh):
    return jax.shard_map(
        functools.partial(per_device, mesh.shape["region"], mesh.shape["tile"]),
        mesh=mesh,
        in_specs=(
            P(("region", "tile"), None),
            P(None, ("region", "tile")),
            P(),
            P(("region", "tile")),
            P(),
        ),
        out_specs=(P(None, ("region", "tile")), P()),
        check_vma=False,
    )
```

```python
import functools

import jax
import jax.numpy as jnp
from jax import lax
from jax.experimental import pallas as pl
from jax.experimental.pallas import tpu as pltpu
from jax.sharding import PartitionSpec as P

BAND = 256
MESH = pl.DeviceIdType.MESH
F32 = jnp.float32
BF16 = jnp.bfloat16
HIGH = lax.Precision.HIGHEST
NT = (((1,), (1,)), ((), ()))
NN = (((1,), (0,)), ((), ()))


def split(value):
    hi = value.astype(BF16)
    lo = (value - hi.astype(F32)).astype(BF16)
    return hi, lo


def kernel(
    n_region, n_tile, owners, width,
    bw_ref, vc_ref, q_ref, sc_hbm, p_hbm,
    out_ref, basis_ref,
    rows, sc_ref, p_ref, acc, parts, edge, head_msg, head_got, z_msg, z_got,
    local, extra, got, got_extra, total, total_extra,
    in_sem, small_sem, m_send, m_recv, z_send, z_recv,
    rs_send, rs_recv, rx_send, rx_recv, ag_send, ag_recv, ax_send, ax_recv,
):
    tokens, feats = rows.shape
    k = p_ref.shape[0]
    count = tokens // BAND
    last = count - 1
    devices = n_region * n_tile
    region, tile = lax.axis_index("region"), lax.axis_index("tile")
    me = region * n_tile + tile
    per_row = feats // width

    def where_is(flat):
        return (lax.div(flat, n_tile), lax.rem(flat, n_tile))

    def span(c):
        if isinstance(c, int):
            return pl.ds(c * BAND, BAND)
        return pl.ds(pl.multiple_of(c * BAND, BAND), BAND)

    def fetch(c):
        return pltpu.make_async_copy(q_ref.at[span(c)], rows.at[span(c)], in_sem.at[c])

    def fetch_small(i):
        source, target = ((sc_hbm, sc_ref), (p_hbm, p_ref))[i]
        return pltpu.make_async_copy(source, target, small_sem.at[i])

    fetch_small(1).start()
    fetch_small(0).start()
    fetch(0).start()
    fetch(last).start()

    @pl.loop(1, last)
    def _(c):
        fetch(c).start()

    barrier = pltpu.get_barrier_semaphore()

    @pl.loop(1, devices)
    def _(d):
        pl.semaphore_signal(
            barrier, inc=1, device_id=where_is(lax.rem(me + d, devices)), device_id_type=MESH
        )

    fetch_small(1).wait()
    hi, lo = split(p_ref[...])
    parts[pl.ds(0, k), :] = hi
    parts[pl.ds(k, k), :] = lo
    acc[...] = jnp.zeros_like(acc)

    valid = vc_ref[0]
    left_width = jnp.where(tile > 0, bw_ref[me], 0)
    right_width = jnp.where(tile < n_tile - 1, bw_ref[jnp.minimum(me + 1, devices - 1)], 0)
    place = lax.broadcasted_iota(jnp.int32, (1, BAND), 1)

    def ones(cond):
        return jnp.where(cond, 1.0, 0.0).astype(F32)

    blocks = sc_ref.shape[0]
    step = feats // blocks

    def restore_block(c, scale, j):
        cols = pl.ds(j * step, step)
        rows[span(c), cols] = (
            rows[span(c), cols].astype(F32) * scale[:, j : j + 1]
        ).astype(BF16)

    def restore(c):
        fetch(c).wait()
        scale = sc_ref[:, span(c)].T
        for j in range(blocks):
            restore_block(c, scale, j)

    def project(c):
        both = lax.dot_general(parts[...], rows[span(c), :], NT, preferred_element_type=F32)
        return both[:k] + both[k:]

    def left_side(weighted, weights):
        hi, lo = split(weighted)
        ones_rows = jnp.broadcast_to(weights, (16, BAND)).astype(BF16)
        return jnp.concatenate([hi, lo, ones_rows], axis=0)

    def gather_update(c, weighted, weights):
        lhs = left_side(weighted, weights)
        acc[...] += lax.dot_general(lhs, rows[span(c), :], NN, preferred_element_type=F32)

    def to_left(src, dst, send, recv):
        return pltpu.make_async_remote_copy(
            src_ref=src.at[0], dst_ref=dst.at[1], send_sem=send.at[0], recv_sem=recv.at[1],
            device_id=(region, jnp.maximum(tile - 1, 0)), device_id_type=MESH,
        )

    def to_right(src, dst, send, recv):
        return pltpu.make_async_remote_copy(
            src_ref=src.at[1], dst_ref=dst.at[0], send_sem=send.at[1], recv_sem=recv.at[0],
            device_id=(region, jnp.minimum(tile + 1, n_tile - 1)), device_id_type=MESH,
        )

    has_left, has_right = tile > 0, tile < n_tile - 1

    def swap_start(src, dst, send, recv):
        @pl.when(has_left)
        def _():
            to_left(src, dst, send, recv).start()

        @pl.when(has_right)
        def _():
            to_right(src, dst, send, recv).start()

    def swap_wait(src, dst, send, recv):
        @pl.when(has_left)
        def _():
            to_left(src, dst, send, recv).wait_send()
            to_right(src, dst, send, recv).wait_recv()

        @pl.when(has_right)
        def _():
            to_right(src, dst, send, recv).wait_send()
            to_left(src, dst, send, recv).wait_recv()

    @pl.when(tile == 0)
    def _():
        head_got[0] = jnp.zeros(head_got.shape[1:], BF16)
        z_got[0] = jnp.zeros(z_got.shape[1:], BF16)

    @pl.when(tile == n_tile - 1)
    def _():
        head_got[1] = jnp.zeros(head_got.shape[1:], BF16)
        z_got[1] = jnp.zeros(z_got.shape[1:], BF16)

    fetch_small(0).wait()
    count_hi = lax.shift_right_logical(valid, 6)
    count_lo = valid - count_hi * 64
    for side, c in ((0, 0), (1, last)):
        restore(c)
        own = project(c)
        edge[side] = own
        hi, lo = split(own)
        head_msg[side, pl.ds(0, k), :] = hi
        head_msg[side, pl.ds(k, k), :] = lo
        head_msg[side, pl.ds(2 * k, 16), :] = jnp.full((16, BAND), count_hi.astype(F32), F32).astype(BF16)
        head_msg[side, pl.ds(2 * k + 16, 16), :] = jnp.full((16, BAND), count_lo.astype(F32), F32).astype(BF16)

    pl.semaphore_wait(barrier, devices - 1)
    swap_start(head_msg, head_got, m_send, m_recv)

    restore(1)
    pieces = blocks // 2
    for c in range(1, last):
        following = c + 1 < last
        if following:
            fetch(c + 1).wait()
            scale = sc_ref[:, span(c + 1)].T
        weights = ones(c * BAND + place < valid)
        weighted = project(c) * weights
        if following:
            for j in range(pieces):
                restore_block(c + 1, scale, j)
        lhs = left_side(weighted, weights)
        for j in range(pieces):
            cols = pl.ds(j * (feats // pieces), feats // pieces)
            acc[:, cols] += lax.dot_general(
                lhs, rows[span(c), cols], NN, preferred_element_type=F32
            )
            if following and pieces + j < blocks:
                restore_block(c + 1, scale, pieces + j)
        if following:
            for j in range(2 * pieces, blocks):
                restore_block(c + 1, scale, j)

    from_row = lax.broadcasted_iota(jnp.int32, (BAND, BAND), 0)
    to_col = lax.broadcasted_iota(jnp.int32, (BAND, BAND), 1)
    shifts = (BAND - left_width, right_width - BAND)
    paired = (place < left_width, place >= BAND - right_width)
    own_valid = (ones(place < valid), ones(tokens - BAND + place < valid))

    def aligned(side, message):
        pick = ones(from_row == to_col + shifts[side]).astype(BF16)
        moved = lax.dot_general(message, pick, NN, preferred_element_type=F32)
        return moved[:k] + moved[k:]

    swap_wait(head_msg, head_got, m_send, m_recv)
    for side, c in ((0, 0), (1, last)):
        other = aligned(side, head_got[side, pl.ds(0, 2 * k), :])
        hi = head_got[side, pl.ds(2 * k, 16), :].astype(F32)
        lo = head_got[side, pl.ds(2 * k + 16, 16), :].astype(F32)
        other_count = (hi * 64.0 + lo)[:1]
        start = tokens - left_width if side == 0 else right_width - BAND
        other_valid = ones((place + start).astype(F32) < other_count)
        both = own_valid[side] + other_valid
        own = edge[side]
        weighted = jnp.where(
            paired[side], (own + other) * (both * 0.25), own * own_valid[side]
        )
        weights = jnp.where(paired[side], both * 0.5, own_valid[side])
        gather_update(c, weighted, weights)

    local[...] = acc[pl.ds(0, k), :] + acc[pl.ds(k, k), :]
    sums = acc[pl.ds(2 * k, 8), :][:1]
    groups = feats // 128
    extra[...] = jnp.concatenate(
        [
            jnp.concatenate([sums[:, i * 128 : (i + 1) * 128] for i in range(groups)], axis=0),
            jnp.full((groups, 128), valid.astype(F32), F32),
        ],
        axis=1,
    )

    def chunk(ref, i):
        return ref.at[
            pl.ds(pl.multiple_of(lax.div(i, per_row) * 8, 8), 8),
            pl.ds(pl.multiple_of(lax.rem(i, per_row) * width, 128), width),
        ]

    def scatter(d):
        target = lax.rem(me + d, devices)
        return pltpu.make_async_remote_copy(
            src_ref=chunk(local, lax.rem(target, owners)), dst_ref=got.at[d - 1],
            send_sem=rs_send.at[d - 1], recv_sem=rs_recv.at[d - 1],
            device_id=where_is(target), device_id_type=MESH,
        )

    def scatter_extra(d):
        return pltpu.make_async_remote_copy(
            src_ref=extra, dst_ref=got_extra.at[d - 1],
            send_sem=rx_send, recv_sem=rx_recv.at[d - 1],
            device_id=where_is(lax.rem(me + d, devices)), device_id_type=MESH,
        )

    def spread(d):
        mine = chunk(total, lax.rem(me, owners))
        return pltpu.make_async_remote_copy(
            src_ref=mine, dst_ref=mine,
            send_sem=ag_send.at[d - 1], recv_sem=ag_recv.at[d - 1],
            device_id=where_is(lax.rem(me + d, devices)), device_id_type=MESH,
        )

    def spread_extra(d):
        return pltpu.make_async_remote_copy(
            src_ref=total_extra, dst_ref=total_extra,
            send_sem=ax_send.at[d - 1], recv_sem=ax_recv,
            device_id=where_is(lax.rem(me + d, devices)), device_id_type=MESH,
        )

    @pl.when(me != 0)
    def _():
        scatter_extra(devices - me).start()

    @pl.loop(1, devices)
    def _(d):
        @pl.when(lax.rem(me + d, devices) < owners)
        def _():
            scatter(d).start()

    @pl.when(me == 0)
    def _():
        @pl.loop(1, devices)
        def _(d):
            scatter_extra(d).wait_recv()

        def add(d, so_far):
            return so_far + got_extra[d]

        total_extra[...] = lax.fori_loop(0, devices - 1, add, extra[...])

        @pl.loop(1, devices)
        def _(d):
            spread_extra(d).start()

    @pl.when(me < owners)
    def _():
        @pl.loop(1, devices)
        def _(d):
            scatter(d).wait_recv()

        def add(d, so_far):
            return so_far + got[d]

        chunk(total, lax.rem(me, owners))[...] = lax.fori_loop(
            0, devices - 1, add, chunk(local, lax.rem(me, owners))[...]
        )

        @pl.loop(1, devices)
        def _(d):
            spread(d).start()

    @pl.when(me != 0)
    def _():
        spread_extra(1).wait_recv()

    @pl.loop(1, devices)
    def _(d):
        @pl.when(lax.rem(me + devices - d, devices) < owners)
        def _():
            spread(d).wait_recv()

    packed = total_extra[...]
    token_count = packed[:1, 128:129]
    sums = jnp.concatenate([packed[i : i + 1, :128] for i in range(groups)], axis=1)
    average = sums / token_count
    mean_image = jnp.sum(p_ref[...] * average, axis=1, keepdims=True)
    update = total[...] - mean_image * sums
    cross = lax.dot_general(update, update, NT, precision=HIGH, preferred_element_type=F32)
    row = lax.broadcasted_iota(jnp.int32, (k, k), 0)
    col = lax.broadcasted_iota(jnp.int32, (k, k), 1)
    work = jnp.concatenate([cross, ones(row == col)], axis=1)
    line = lax.broadcasted_iota(jnp.int32, (k, 1), 0)
    group = 4
    for first in range(0, k, group):
        wide = [
            jnp.broadcast_to(work[:, i : i + 1], (k, 2 * k))
            for i in range(first, first + group)
        ]
        for j in range(group):
            i = first + j
            below = jnp.where(line > i, wide[j], 0.0)
            turn = 1.0 / wide[j][i : i + 1, :]
            for l in range(j + 1, group):
                wide[l] = wide[l] - below * (wide[l][i : i + 1, :] * turn)
            work = work - below * (work[i : i + 1, :] * turn)
    diagonal = jnp.sum(jnp.where(row == col, work[:, :k], 0.0), axis=1, keepdims=True)
    inverse = work[:, k:] / jnp.sqrt(diagonal)
    new_t = lax.dot_general(inverse, update, NN, precision=HIGH, preferred_element_type=F32)
    basis_ref[...] = new_t
    shift = jnp.sum(new_t * average, axis=1, keepdims=True)
    hi, lo = split(new_t)
    parts[pl.ds(0, k), :] = hi
    parts[pl.ds(k, k), :] = lo

    for side, c in ((0, 0), (1, last)):
        own = project(c)
        edge[side] = own
        hi, lo = split(own)
        z_msg[side, pl.ds(0, k), :] = hi
        z_msg[side, pl.ds(k, k), :] = lo
    swap_start(z_msg, z_got, z_send, z_recv)

    @pl.loop(1, last)
    def _(c):
        usable = c * BAND + place < valid
        out_ref[:, span(c)] = jnp.where(usable, project(c) - shift, 0.0)

    swap_wait(z_msg, z_got, z_send, z_recv)
    for side, c in ((0, 0), (1, last)):
        other = aligned(side, z_got[side])
        own = edge[side]
        mixed = jnp.where(paired[side], (own + other) * 0.5, own)
        out_ref[:, span(c)] = jnp.where(own_valid[side] > 0.5, mixed - shift, 0.0)

    @pl.when(me != 0)
    def _():
        scatter_extra(devices - me).wait_send()

    @pl.when(me == 0)
    def _():
        @pl.loop(1, devices)
        def _(d):
            spread_extra(d).wait_send()

    @pl.when(me < owners)
    def _():
        @pl.loop(1, devices)
        def _(d):
            spread(d).wait_send()

    @pl.loop(1, devices)
    def _(d):
        @pl.when(lax.rem(me + d, devices) < owners)
        def _():
            scatter(d).wait_send()


def per_device(n_region, n_tile, quantized, block_scales, band_width, valid_count, prior_basis):
    tokens, feats = quantized.shape
    k = prior_basis.shape[1]
    devices = n_region * n_tile
    tiles = (k // 8) * (feats // 128)
    owners = min(devices, tiles)
    width = 128 * (tiles // owners)
    others = devices - 1
    dma = pltpu.SemaphoreType.DMA
    vmem = pl.BlockSpec(memory_space=pltpu.VMEM)
    smem = pl.BlockSpec(memory_space=pltpu.SMEM)
    projected, basis = pl.pallas_call(
        functools.partial(kernel, n_region, n_tile, owners, width),
        out_shape=(
            jax.ShapeDtypeStruct((k, tokens), F32),
            jax.ShapeDtypeStruct((k, feats), F32),
        ),
        in_specs=[smem, smem] + [pl.BlockSpec(memory_space=pltpu.HBM)] * 3,
        out_specs=(vmem, vmem),
        scratch_shapes=[
            pltpu.VMEM((tokens, feats), BF16),
            pltpu.VMEM(block_scales.shape, F32),
            pltpu.VMEM((k, feats), F32),
            pltpu.VMEM((2 * k + 16, feats), F32),
            pltpu.VMEM((2 * k, feats), BF16),
            pltpu.VMEM((2, k, BAND), F32),
            pltpu.VMEM((2, 2 * k + 32, BAND), BF16),
            pltpu.VMEM((2, 2 * k + 32, BAND), BF16),
            pltpu.VMEM((2, 2 * k, BAND), BF16),
            pltpu.VMEM((2, 2 * k, BAND), BF16),
            pltpu.VMEM((k, feats), F32),
            pltpu.VMEM((feats // 128, 256), F32),
            pltpu.VMEM((others, 8, width), F32),
            pltpu.VMEM((others, feats // 128, 256), F32),
            pltpu.VMEM((k, feats), F32),
            pltpu.VMEM((feats // 128, 256), F32),
            dma((tokens // BAND,)), dma((2,)),
            dma((2,)), dma((2,)), dma((2,)), dma((2,)),
            dma((others,)), dma((others,)), dma(()), dma((others,)),
            dma((others,)), dma((others,)), dma((others,)), dma(()),
        ],
        compiler_params=pltpu.CompilerParams(
            collective_id=0, has_side_effects=True, vmem_limit_bytes=48 * 1024 * 1024
        ),
    )(band_width, valid_count, quantized, block_scales, prior_basis.T)
    return projected, basis.T


def solution(mesh):
    return jax.shard_map(
        functools.partial(per_device, mesh.shape["region"], mesh.shape["tile"]),
        mesh=mesh,
        in_specs=(
            P(("region", "tile"), None),
            P(None, ("region", "tile")),
            P(),
            P(("region", "tile")),
            P(),
        ),
        out_specs=(P(None, ("region", "tile")), P()),
        check_vma=False,
    )
```

```python
import functools

import jax
import jax.numpy as jnp
from jax import lax
from jax.experimental import pallas as pl
from jax.experimental.pallas import tpu as pltpu
from jax.sharding import PartitionSpec as P

BAND = 256
MESH = pl.DeviceIdType.MESH
F32 = jnp.float32
BF16 = jnp.bfloat16
HIGH = lax.Precision.HIGHEST
NT = (((1,), (1,)), ((), ()))
NN = (((1,), (0,)), ((), ()))


def split(value):
    hi = value.astype(BF16)
    lo = (value - hi.astype(F32)).astype(BF16)
    return hi, lo


def kernel(
    n_region, n_tile, owners, width,
    bw_ref, vc_ref, q_ref, sc_hbm, p_hbm,
    out_hbm, basis_ref,
    out_ref,
    rows, sc_ref, p_ref, acc, parts, edge, head_msg, head_got, z_msg, z_got,
    local, extra, got, got_extra, total, total_extra,
    in_sem, small_sem, out_sem, m_send, m_recv, z_send, z_recv,
    rs_send, rs_recv, rx_send, rx_recv, ag_send, ag_recv, ax_send, ax_recv,
):
    tokens, feats = rows.shape
    k = p_ref.shape[0]
    count = tokens // BAND
    last = count - 1
    devices = n_region * n_tile
    region, tile = lax.axis_index("region"), lax.axis_index("tile")
    me = region * n_tile + tile
    per_row = feats // width

    def where_is(flat):
        return (lax.div(flat, n_tile), lax.rem(flat, n_tile))

    def span(c):
        if isinstance(c, int):
            return pl.ds(c * BAND, BAND)
        return pl.ds(pl.multiple_of(c * BAND, BAND), BAND)

    def fetch(c):
        return pltpu.make_async_copy(q_ref.at[span(c)], rows.at[span(c)], in_sem.at[c])

    def fetch_small(i):
        source, target = ((sc_hbm, sc_ref), (p_hbm, p_ref))[i]
        return pltpu.make_async_copy(source, target, small_sem.at[i])

    fetch_small(1).start()
    fetch_small(0).start()
    fetch(0).start()
    fetch(last).start()

    @pl.loop(1, last)
    def _(c):
        fetch(c).start()

    def put(c):
        return pltpu.make_async_copy(
            out_ref.at[:, span(c)], out_hbm.at[:, span(c)], out_sem.at[c]
        )

    barrier = pltpu.get_barrier_semaphore()

    @pl.loop(1, devices)
    def _(d):
        pl.semaphore_signal(
            barrier, inc=1, device_id=where_is(lax.rem(me + d, devices)), device_id_type=MESH
        )

    fetch_small(1).wait()
    hi, lo = split(p_ref[...])
    parts[pl.ds(0, k), :] = hi
    parts[pl.ds(k, k), :] = lo
    acc[...] = jnp.zeros_like(acc)

    valid = vc_ref[0]
    left_width = jnp.where(tile > 0, bw_ref[me], 0)
    right_width = jnp.where(tile < n_tile - 1, bw_ref[jnp.minimum(me + 1, devices - 1)], 0)
    place = lax.broadcasted_iota(jnp.int32, (1, BAND), 1)

    def ones(cond):
        return jnp.where(cond, 1.0, 0.0).astype(F32)

    blocks = sc_ref.shape[0]
    step = feats // blocks

    def restore_block(c, scale, j):
        cols = pl.ds(j * step, step)
        rows[span(c), cols] = (
            rows[span(c), cols].astype(F32) * scale[:, j : j + 1]
        ).astype(BF16)

    def restore(c):
        fetch(c).wait()
        scale = sc_ref[:, span(c)].T
        for j in range(blocks):
            restore_block(c, scale, j)

    def project(c):
        both = lax.dot_general(parts[...], rows[span(c), :], NT, preferred_element_type=F32)
        return both[:k] + both[k:]

    def left_side(weighted, weights):
        hi, lo = split(weighted)
        ones_rows = jnp.broadcast_to(weights, (16, BAND)).astype(BF16)
        return jnp.concatenate([hi, lo, ones_rows], axis=0)

    def gather_update(c, weighted, weights):
        lhs = left_side(weighted, weights)
        acc[...] += lax.dot_general(lhs, rows[span(c), :], NN, preferred_element_type=F32)

    def to_left(src, dst, send, recv):
        return pltpu.make_async_remote_copy(
            src_ref=src.at[0], dst_ref=dst.at[1], send_sem=send.at[0], recv_sem=recv.at[1],
            device_id=(region, jnp.maximum(tile - 1, 0)), device_id_type=MESH,
        )

    def to_right(src, dst, send, recv):
        return pltpu.make_async_remote_copy(
            src_ref=src.at[1], dst_ref=dst.at[0], send_sem=send.at[1], recv_sem=recv.at[0],
            device_id=(region, jnp.minimum(tile + 1, n_tile - 1)), device_id_type=MESH,
        )

    has_left, has_right = tile > 0, tile < n_tile - 1

    def swap_start(src, dst, send, recv):
        @pl.when(has_left)
        def _():
            to_left(src, dst, send, recv).start()

        @pl.when(has_right)
        def _():
            to_right(src, dst, send, recv).start()

    def swap_wait(src, dst, send, recv):
        @pl.when(has_left)
        def _():
            to_left(src, dst, send, recv).wait_send()
            to_right(src, dst, send, recv).wait_recv()

        @pl.when(has_right)
        def _():
            to_right(src, dst, send, recv).wait_send()
            to_left(src, dst, send, recv).wait_recv()

    @pl.when(tile == 0)
    def _():
        head_got[0] = jnp.zeros(head_got.shape[1:], BF16)
        z_got[0] = jnp.zeros(z_got.shape[1:], BF16)

    @pl.when(tile == n_tile - 1)
    def _():
        head_got[1] = jnp.zeros(head_got.shape[1:], BF16)
        z_got[1] = jnp.zeros(z_got.shape[1:], BF16)

    fetch_small(0).wait()
    count_hi = lax.shift_right_logical(valid, 6)
    count_lo = valid - count_hi * 64
    def send_edge(side, own):
        edge[side] = own
        hi, lo = split(own)
        whole = (16, BAND)
        head_msg[side, pl.ds(0, k), :] = hi
        head_msg[side, pl.ds(k, k), :] = lo
        head_msg[side, pl.ds(2 * k, 16), :] = jnp.full(whole, count_hi.astype(F32), F32).astype(BF16)
        head_msg[side, pl.ds(2 * k + 16, 16), :] = jnp.full(whole, count_lo.astype(F32), F32).astype(BF16)

    restore(0)
    pieces = blocks // 2
    order = [0, last] + list(range(1, last))
    for at, c in enumerate(order):
        following = order[at + 1] if at + 1 < count else None
        if following is not None:
            fetch(following).wait()
            scale = sc_ref[:, span(following)].T
        own = project(c)
        if c in (0, last):
            for j in range(blocks):
                restore_block(following, scale, j)
            send_edge(0 if c == 0 else 1, own)
            if c == last:
                pl.semaphore_wait(barrier, devices - 1)
                swap_start(head_msg, head_got, m_send, m_recv)
            continue
        weights = ones(c * BAND + place < valid)
        if following is not None:
            for j in range(pieces):
                restore_block(following, scale, j)
        lhs = left_side(own * weights, weights)
        for j in range(pieces):
            cols = pl.ds(j * (feats // pieces), feats // pieces)
            acc[:, cols] += lax.dot_general(
                lhs, rows[span(c), cols], NN, preferred_element_type=F32
            )
            if following is not None:
                restore_block(following, scale, pieces + j)
        if following is not None:
            for j in range(2 * pieces, blocks):
                restore_block(following, scale, j)

    from_row = lax.broadcasted_iota(jnp.int32, (BAND, BAND), 0)
    to_col = lax.broadcasted_iota(jnp.int32, (BAND, BAND), 1)
    shifts = (BAND - left_width, right_width - BAND)
    paired = (place < left_width, place >= BAND - right_width)
    own_valid = (ones(place < valid), ones(tokens - BAND + place < valid))

    def aligned(side, message):
        pick = ones(from_row == to_col + shifts[side]).astype(BF16)
        moved = lax.dot_general(message, pick, NN, preferred_element_type=F32)
        return moved[:k] + moved[k:]

    swap_wait(head_msg, head_got, m_send, m_recv)
    for side, c in ((0, 0), (1, last)):
        other = aligned(side, head_got[side, pl.ds(0, 2 * k), :])
        hi = head_got[side, pl.ds(2 * k, 16), :].astype(F32)
        lo = head_got[side, pl.ds(2 * k + 16, 16), :].astype(F32)
        other_count = (hi * 64.0 + lo)[:1]
        start = tokens - left_width if side == 0 else right_width - BAND
        other_valid = ones((place + start).astype(F32) < other_count)
        both = own_valid[side] + other_valid
        own = edge[side]
        weighted = jnp.where(
            paired[side], (own + other) * (both * 0.25), own * own_valid[side]
        )
        weights = jnp.where(paired[side], both * 0.5, own_valid[side])
        gather_update(c, weighted, weights)

    local[...] = acc[pl.ds(0, k), :] + acc[pl.ds(k, k), :]
    sums = acc[pl.ds(2 * k, 8), :][:1]
    groups = feats // 128
    extra[...] = jnp.concatenate(
        [
            jnp.concatenate([sums[:, i * 128 : (i + 1) * 128] for i in range(groups)], axis=0),
            jnp.full((groups, 128), valid.astype(F32), F32),
        ],
        axis=1,
    )

    def chunk(ref, i):
        return ref.at[
            pl.ds(pl.multiple_of(lax.div(i, per_row) * 8, 8), 8),
            pl.ds(pl.multiple_of(lax.rem(i, per_row) * width, 128), width),
        ]

    def scatter(d):
        target = lax.rem(me + d, devices)
        return pltpu.make_async_remote_copy(
            src_ref=chunk(local, lax.rem(target, owners)), dst_ref=got.at[d - 1],
            send_sem=rs_send.at[d - 1], recv_sem=rs_recv.at[d - 1],
            device_id=where_is(target), device_id_type=MESH,
        )

    def scatter_extra(d):
        return pltpu.make_async_remote_copy(
            src_ref=extra, dst_ref=got_extra.at[d - 1],
            send_sem=rx_send, recv_sem=rx_recv.at[d - 1],
            device_id=where_is(lax.rem(me + d, devices)), device_id_type=MESH,
        )

    def spread(d):
        mine = chunk(total, lax.rem(me, owners))
        return pltpu.make_async_remote_copy(
            src_ref=mine, dst_ref=mine,
            send_sem=ag_send.at[d - 1], recv_sem=ag_recv.at[d - 1],
            device_id=where_is(lax.rem(me + d, devices)), device_id_type=MESH,
        )

    def spread_extra(d):
        return pltpu.make_async_remote_copy(
            src_ref=total_extra, dst_ref=total_extra,
            send_sem=ax_send.at[d - 1], recv_sem=ax_recv,
            device_id=where_is(lax.rem(me + d, devices)), device_id_type=MESH,
        )

    @pl.when(me != 0)
    def _():
        scatter_extra(devices - me).start()

    @pl.loop(1, devices)
    def _(d):
        @pl.when(lax.rem(me + d, devices) < owners)
        def _():
            scatter(d).start()

    @pl.when(me == 0)
    def _():
        @pl.loop(1, devices)
        def _(d):
            scatter_extra(d).wait_recv()

        def add(d, so_far):
            return so_far + got_extra[d]

        total_extra[...] = lax.fori_loop(0, devices - 1, add, extra[...])

        @pl.loop(1, devices)
        def _(d):
            spread_extra(d).start()

    @pl.when(me < owners)
    def _():
        @pl.loop(1, devices)
        def _(d):
            scatter(d).wait_recv()

        def add(d, so_far):
            return so_far + got[d]

        chunk(total, lax.rem(me, owners))[...] = lax.fori_loop(
            0, devices - 1, add, chunk(local, lax.rem(me, owners))[...]
        )

        @pl.loop(1, devices)
        def _(d):
            spread(d).start()

    @pl.when(me != 0)
    def _():
        spread_extra(1).wait_recv()

    @pl.loop(1, devices)
    def _(d):
        @pl.when(lax.rem(me + devices - d, devices) < owners)
        def _():
            spread(d).wait_recv()

    packed = total_extra[...]
    token_count = packed[:1, 128:129]
    sums = jnp.concatenate([packed[i : i + 1, :128] for i in range(groups)], axis=1)
    average = sums / token_count
    mean_image = jnp.sum(p_ref[...] * average, axis=1, keepdims=True)
    update = total[...] - mean_image * sums
    cross = lax.dot_general(update, update, NT, precision=HIGH, preferred_element_type=F32)
    row = lax.broadcasted_iota(jnp.int32, (k, k), 0)
    col = lax.broadcasted_iota(jnp.int32, (k, k), 1)
    work = jnp.concatenate([cross, ones(row == col)], axis=1)
    line = lax.broadcasted_iota(jnp.int32, (k, 1), 0)
    group = 4
    for first in range(0, k, group):
        wide = [
            jnp.broadcast_to(work[:, i : i + 1], (k, 2 * k))
            for i in range(first, first + group)
        ]
        for j in range(group):
            i = first + j
            below = jnp.where(line > i, wide[j], 0.0)
            turn = 1.0 / wide[j][i : i + 1, :]
            for l in range(j + 1, group):
                wide[l] = wide[l] - below * (wide[l][i : i + 1, :] * turn)
            work = work - below * (work[i : i + 1, :] * turn)
    diagonal = jnp.sum(jnp.where(row == col, work[:, :k], 0.0), axis=1, keepdims=True)
    inverse = work[:, k:] / jnp.sqrt(diagonal)
    new_t = lax.dot_general(inverse, update, NN, precision=HIGH, preferred_element_type=F32)
    basis_ref[...] = new_t
    shift = jnp.sum(new_t * average, axis=1, keepdims=True)
    hi, lo = split(new_t)
    parts[pl.ds(0, k), :] = hi
    parts[pl.ds(k, k), :] = lo

    for side, c in ((0, 0), (1, last)):
        own = project(c)
        edge[side] = own
        hi, lo = split(own)
        z_msg[side, pl.ds(0, k), :] = hi
        z_msg[side, pl.ds(k, k), :] = lo
    swap_start(z_msg, z_got, z_send, z_recv)

    @pl.loop(1, last)
    def _(c):
        usable = c * BAND + place < valid
        out_ref[:, span(c)] = jnp.where(usable, project(c) - shift, 0.0)
        put(c).start()

    swap_wait(z_msg, z_got, z_send, z_recv)
    for side, c in ((0, 0), (1, last)):
        other = aligned(side, z_got[side])
        own = edge[side]
        mixed = jnp.where(paired[side], (own + other) * 0.5, own)
        out_ref[:, span(c)] = jnp.where(own_valid[side] > 0.5, mixed - shift, 0.0)
        put(c).start()

    @pl.when(me != 0)
    def _():
        scatter_extra(devices - me).wait_send()

    @pl.when(me == 0)
    def _():
        @pl.loop(1, devices)
        def _(d):
            spread_extra(d).wait_send()

    @pl.when(me < owners)
    def _():
        @pl.loop(1, devices)
        def _(d):
            spread(d).wait_send()

    @pl.loop(1, devices)
    def _(d):
        @pl.when(lax.rem(me + d, devices) < owners)
        def _():
            scatter(d).wait_send()

    @pl.loop(0, count)
    def _(c):
        put(c).wait()


def per_device(n_region, n_tile, quantized, block_scales, band_width, valid_count, prior_basis):
    tokens, feats = quantized.shape
    k = prior_basis.shape[1]
    devices = n_region * n_tile
    tiles = (k // 8) * (feats // 128)
    owners = min(devices, tiles)
    width = 128 * (tiles // owners)
    others = devices - 1
    dma = pltpu.SemaphoreType.DMA
    vmem = pl.BlockSpec(memory_space=pltpu.VMEM)
    smem = pl.BlockSpec(memory_space=pltpu.SMEM)
    projected, basis = pl.pallas_call(
        functools.partial(kernel, n_region, n_tile, owners, width),
        out_shape=(
            jax.ShapeDtypeStruct((k, tokens), F32),
            jax.ShapeDtypeStruct((k, feats), F32),
        ),
        in_specs=[smem, smem] + [pl.BlockSpec(memory_space=pltpu.HBM)] * 3,
        out_specs=(pl.BlockSpec(memory_space=pl.ANY), vmem),
        scratch_shapes=[
            pltpu.VMEM((k, tokens), F32),
            pltpu.VMEM((tokens, feats), BF16),
            pltpu.VMEM(block_scales.shape, F32),
            pltpu.VMEM((k, feats), F32),
            pltpu.VMEM((2 * k + 16, feats), F32),
            pltpu.VMEM((2 * k, feats), BF16),
            pltpu.VMEM((2, k, BAND), F32),
            pltpu.VMEM((2, 2 * k + 32, BAND), BF16),
            pltpu.VMEM((2, 2 * k + 32, BAND), BF16),
            pltpu.VMEM((2, 2 * k, BAND), BF16),
            pltpu.VMEM((2, 2 * k, BAND), BF16),
            pltpu.VMEM((k, feats), F32),
            pltpu.VMEM((feats // 128, 256), F32),
            pltpu.VMEM((others, 8, width), F32),
            pltpu.VMEM((others, feats // 128, 256), F32),
            pltpu.VMEM((k, feats), F32),
            pltpu.VMEM((feats // 128, 256), F32),
            dma((tokens // BAND,)), dma((2,)), dma((tokens // BAND,)),
            dma((2,)), dma((2,)), dma((2,)), dma((2,)),
            dma((others,)), dma((others,)), dma(()), dma((others,)),
            dma((others,)), dma((others,)), dma((others,)), dma(()),
        ],
        compiler_params=pltpu.CompilerParams(
            collective_id=0, has_side_effects=True, vmem_limit_bytes=67043328
        ),
    )(band_width, valid_count, quantized, block_scales, prior_basis.T)
    return projected, basis.T


def solution(mesh):
    return jax.shard_map(
        functools.partial(per_device, mesh.shape["region"], mesh.shape["tile"]),
        mesh=mesh,
        in_specs=(
            P(("region", "tile"), None),
            P(None, ("region", "tile")),
            P(),
            P(("region", "tile")),
            P(),
        ),
        out_specs=(P(None, ("region", "tile")), P()),
        check_vma=False,
    )
```

```python
import functools

import jax
import jax.numpy as jnp
from jax import lax
from jax.experimental import pallas as pl
from jax.experimental.pallas import tpu as pltpu
from jax.sharding import PartitionSpec as P

BAND = 256
MESH = pl.DeviceIdType.MESH
F32 = jnp.float32
BF16 = jnp.bfloat16
HIGH = lax.Precision.HIGHEST
NT = (((1,), (1,)), ((), ()))
NN = (((1,), (0,)), ((), ()))


def split(value):
    hi = value.astype(BF16)
    lo = (value - hi.astype(F32)).astype(BF16)
    return hi, lo


def kernel(
    n_region, n_tile, owners, width,
    bw_ref, vc_ref, q_ref, sc_ref, p_ref,
    out_ref, basis_ref,
    rows, acc, parts, edge, head_msg, head_got, z_msg, z_got,
    local, extra, got, got_extra, total, total_extra,
    in_sem, m_send, m_recv, z_send, z_recv,
    rs_send, rs_recv, rx_send, rx_recv, ag_send, ag_recv, ax_send, ax_recv,
):
    tokens, feats = rows.shape
    k = p_ref.shape[0]
    count = tokens // BAND
    last = count - 1
    devices = n_region * n_tile
    region, tile = lax.axis_index("region"), lax.axis_index("tile")
    me = region * n_tile + tile
    per_row = feats // width

    def where_is(flat):
        return (lax.div(flat, n_tile), lax.rem(flat, n_tile))

    def span(c):
        if isinstance(c, int):
            return pl.ds(c * BAND, BAND)
        return pl.ds(pl.multiple_of(c * BAND, BAND), BAND)

    def fetch(c):
        return pltpu.make_async_copy(q_ref.at[span(c)], rows.at[span(c)], in_sem.at[c])

    fetch(0).start()
    fetch(last).start()

    @pl.loop(1, last)
    def _(c):
        fetch(c).start()

    barrier = pltpu.get_barrier_semaphore()

    @pl.loop(1, devices)
    def _(d):
        pl.semaphore_signal(
            barrier, inc=1, device_id=where_is(lax.rem(me + d, devices)), device_id_type=MESH
        )

    hi, lo = split(p_ref[...])
    parts[pl.ds(0, k), :] = hi
    parts[pl.ds(k, k), :] = lo
    acc[...] = jnp.zeros_like(acc)

    valid = vc_ref[0]
    left_width = jnp.where(tile > 0, bw_ref[me], 0)
    right_width = jnp.where(tile < n_tile - 1, bw_ref[jnp.minimum(me + 1, devices - 1)], 0)
    place = lax.broadcasted_iota(jnp.int32, (1, BAND), 1)

    def ones(cond):
        return jnp.where(cond, 1.0, 0.0).astype(F32)

    blocks = sc_ref.shape[0]
    step = feats // blocks

    def restore_block(c, scale, j):
        cols = pl.ds(j * step, step)
        rows[span(c), cols] = (
            rows[span(c), cols].astype(F32) * scale[:, j : j + 1]
        ).astype(BF16)

    def restore(c):
        fetch(c).wait()
        scale = sc_ref[:, span(c)].T
        for j in range(blocks):
            restore_block(c, scale, j)

    def project(c):
        both = lax.dot_general(parts[...], rows[span(c), :], NT, preferred_element_type=F32)
        return both[:k] + both[k:]

    def left_side(weighted, weights):
        hi, lo = split(weighted)
        ones_rows = jnp.broadcast_to(weights, (16, BAND)).astype(BF16)
        return jnp.concatenate([hi, lo, ones_rows], axis=0)

    def gather_update(c, weighted, weights):
        lhs = left_side(weighted, weights)
        acc[...] += lax.dot_general(lhs, rows[span(c), :], NN, preferred_element_type=F32)

    def to_left(src, dst, send, recv):
        return pltpu.make_async_remote_copy(
            src_ref=src.at[0], dst_ref=dst.at[1], send_sem=send.at[0], recv_sem=recv.at[1],
            device_id=(region, jnp.maximum(tile - 1, 0)), device_id_type=MESH,
        )

    def to_right(src, dst, send, recv):
        return pltpu.make_async_remote_copy(
            src_ref=src.at[1], dst_ref=dst.at[0], send_sem=send.at[1], recv_sem=recv.at[0],
            device_id=(region, jnp.minimum(tile + 1, n_tile - 1)), device_id_type=MESH,
        )

    has_left, has_right = tile > 0, tile < n_tile - 1

    def swap_start(src, dst, send, recv):
        @pl.when(has_left)
        def _():
            to_left(src, dst, send, recv).start()

        @pl.when(has_right)
        def _():
            to_right(src, dst, send, recv).start()

    def swap_wait(src, dst, send, recv):
        @pl.when(has_left)
        def _():
            to_left(src, dst, send, recv).wait_send()
            to_right(src, dst, send, recv).wait_recv()

        @pl.when(has_right)
        def _():
            to_right(src, dst, send, recv).wait_send()
            to_left(src, dst, send, recv).wait_recv()

    @pl.when(tile == 0)
    def _():
        head_got[0] = jnp.zeros(head_got.shape[1:], BF16)
        z_got[0] = jnp.zeros(z_got.shape[1:], BF16)

    @pl.when(tile == n_tile - 1)
    def _():
        head_got[1] = jnp.zeros(head_got.shape[1:], BF16)
        z_got[1] = jnp.zeros(z_got.shape[1:], BF16)

    count_hi = lax.shift_right_logical(valid, 6)
    count_lo = valid - count_hi * 64
    def send_edge(side, own):
        edge[side] = own
        hi, lo = split(own)
        whole = (16, BAND)
        head_msg[side, pl.ds(0, k), :] = hi
        head_msg[side, pl.ds(k, k), :] = lo
        head_msg[side, pl.ds(2 * k, 16), :] = jnp.full(whole, count_hi.astype(F32), F32).astype(BF16)
        head_msg[side, pl.ds(2 * k + 16, 16), :] = jnp.full(whole, count_lo.astype(F32), F32).astype(BF16)

    restore(0)
    pieces = blocks // 2
    order = [0, last] + list(range(1, last))
    for at, c in enumerate(order):
        following = order[at + 1] if at + 1 < count else None
        if following is not None:
            fetch(following).wait()
            scale = sc_ref[:, span(following)].T
        own = project(c)
        if c in (0, last):
            for j in range(blocks):
                restore_block(following, scale, j)
            send_edge(0 if c == 0 else 1, own)
            if c == last:
                pl.semaphore_wait(barrier, devices - 1)
                swap_start(head_msg, head_got, m_send, m_recv)
            continue
        weights = ones(c * BAND + place < valid)
        if following is not None:
            for j in range(pieces):
                restore_block(following, scale, j)
        lhs = left_side(own * weights, weights)
        for j in range(pieces):
            cols = pl.ds(j * (feats // pieces), feats // pieces)
            acc[:, cols] += lax.dot_general(
                lhs, rows[span(c), cols], NN, preferred_element_type=F32
            )
            if following is not None:
                restore_block(following, scale, pieces + j)
        if following is not None:
            for j in range(2 * pieces, blocks):
                restore_block(following, scale, j)

    from_row = lax.broadcasted_iota(jnp.int32, (BAND, BAND), 0)
    to_col = lax.broadcasted_iota(jnp.int32, (BAND, BAND), 1)
    shifts = (BAND - left_width, right_width - BAND)
    paired = (place < left_width, place >= BAND - right_width)
    own_valid = (ones(place < valid), ones(tokens - BAND + place < valid))

    def aligned(side, message):
        pick = ones(from_row == to_col + shifts[side]).astype(BF16)
        moved = lax.dot_general(message, pick, NN, preferred_element_type=F32)
        return moved[:k] + moved[k:]

    swap_wait(head_msg, head_got, m_send, m_recv)
    for side, c in ((0, 0), (1, last)):
        other = aligned(side, head_got[side, pl.ds(0, 2 * k), :])
        hi = head_got[side, pl.ds(2 * k, 16), :].astype(F32)
        lo = head_got[side, pl.ds(2 * k + 16, 16), :].astype(F32)
        other_count = (hi * 64.0 + lo)[:1]
        start = tokens - left_width if side == 0 else right_width - BAND
        other_valid = ones((place + start).astype(F32) < other_count)
        both = own_valid[side] + other_valid
        own = edge[side]
        weighted = jnp.where(
            paired[side], (own + other) * (both * 0.25), own * own_valid[side]
        )
        weights = jnp.where(paired[side], both * 0.5, own_valid[side])
        gather_update(c, weighted, weights)

    local[...] = acc[pl.ds(0, k), :] + acc[pl.ds(k, k), :]
    sums = acc[pl.ds(2 * k, 8), :][:1]
    groups = feats // 128
    extra[...] = jnp.concatenate(
        [
            jnp.concatenate([sums[:, i * 128 : (i + 1) * 128] for i in range(groups)], axis=0),
            jnp.full((groups, 128), valid.astype(F32), F32),
        ],
        axis=1,
    )

    def chunk(ref, i):
        return ref.at[
            pl.ds(pl.multiple_of(lax.div(i, per_row) * 8, 8), 8),
            pl.ds(pl.multiple_of(lax.rem(i, per_row) * width, 128), width),
        ]

    def scatter(d):
        target = lax.rem(me + d, devices)
        return pltpu.make_async_remote_copy(
            src_ref=chunk(local, lax.rem(target, owners)), dst_ref=got.at[d - 1],
            send_sem=rs_send.at[d - 1], recv_sem=rs_recv.at[d - 1],
            device_id=where_is(target), device_id_type=MESH,
        )

    def scatter_extra(d):
        return pltpu.make_async_remote_copy(
            src_ref=extra, dst_ref=got_extra.at[d - 1],
            send_sem=rx_send, recv_sem=rx_recv.at[d - 1],
            device_id=where_is(lax.rem(me + d, devices)), device_id_type=MESH,
        )

    def spread(d):
        mine = chunk(total, lax.rem(me, owners))
        return pltpu.make_async_remote_copy(
            src_ref=mine, dst_ref=mine,
            send_sem=ag_send.at[d - 1], recv_sem=ag_recv.at[d - 1],
            device_id=where_is(lax.rem(me + d, devices)), device_id_type=MESH,
        )

    def spread_extra(d):
        return pltpu.make_async_remote_copy(
            src_ref=total_extra, dst_ref=total_extra,
            send_sem=ax_send.at[d - 1], recv_sem=ax_recv,
            device_id=where_is(lax.rem(me + d, devices)), device_id_type=MESH,
        )

    @pl.when(me != 0)
    def _():
        scatter_extra(devices - me).start()

    @pl.loop(1, devices)
    def _(d):
        @pl.when(lax.rem(me + d, devices) < owners)
        def _():
            scatter(d).start()

    @pl.when(me == 0)
    def _():
        @pl.loop(1, devices)
        def _(d):
            scatter_extra(d).wait_recv()

        def add(d, so_far):
            return so_far + got_extra[d]

        total_extra[...] = lax.fori_loop(0, devices - 1, add, extra[...])

        @pl.loop(1, devices)
        def _(d):
            spread_extra(d).start()

    @pl.when(me < owners)
    def _():
        @pl.loop(1, devices)
        def _(d):
            scatter(d).wait_recv()

        def add(d, so_far):
            return so_far + got[d]

        chunk(total, lax.rem(me, owners))[...] = lax.fori_loop(
            0, devices - 1, add, chunk(local, lax.rem(me, owners))[...]
        )

        @pl.loop(1, devices)
        def _(d):
            spread(d).start()

    @pl.when(me != 0)
    def _():
        spread_extra(1).wait_recv()

    @pl.loop(1, devices)
    def _(d):
        @pl.when(lax.rem(me + devices - d, devices) < owners)
        def _():
            spread(d).wait_recv()

    packed = total_extra[...]
    token_count = packed[:1, 128:129]
    sums = jnp.concatenate([packed[i : i + 1, :128] for i in range(groups)], axis=1)
    average = sums / token_count
    mean_image = jnp.sum(p_ref[...] * average, axis=1, keepdims=True)
    update = total[...] - mean_image * sums
    cross = lax.dot_general(update, update, NT, precision=HIGH, preferred_element_type=F32)
    row = lax.broadcasted_iota(jnp.int32, (k, k), 0)
    col = lax.broadcasted_iota(jnp.int32, (k, k), 1)
    work = jnp.concatenate([cross, ones(row == col)], axis=1)
    line = lax.broadcasted_iota(jnp.int32, (k, 1), 0)
    group = 4
    for first in range(0, k, group):
        wide = [
            jnp.broadcast_to(work[:, i : i + 1], (k, 2 * k))
            for i in range(first, first + group)
        ]
        for j in range(group):
            i = first + j
            below = jnp.where(line > i, wide[j], 0.0)
            turn = 1.0 / wide[j][i : i + 1, :]
            for l in range(j + 1, group):
                wide[l] = wide[l] - below * (wide[l][i : i + 1, :] * turn)
            work = work - below * (work[i : i + 1, :] * turn)
    diagonal = jnp.sum(jnp.where(row == col, work[:, :k], 0.0), axis=1, keepdims=True)
    inverse = work[:, k:] / jnp.sqrt(diagonal)
    new_t = lax.dot_general(inverse, update, NN, precision=HIGH, preferred_element_type=F32)
    basis_ref[...] = new_t
    shift = jnp.sum(new_t * average, axis=1, keepdims=True)
    hi, lo = split(new_t)
    parts[pl.ds(0, k), :] = hi
    parts[pl.ds(k, k), :] = lo

    for side, c in ((0, 0), (1, last)):
        own = project(c)
        edge[side] = own
        hi, lo = split(own)
        z_msg[side, pl.ds(0, k), :] = hi
        z_msg[side, pl.ds(k, k), :] = lo
    swap_start(z_msg, z_got, z_send, z_recv)

    @pl.loop(1, last)
    def _(c):
        usable = c * BAND + place < valid
        out_ref[:, span(c)] = jnp.where(usable, project(c) - shift, 0.0)

    swap_wait(z_msg, z_got, z_send, z_recv)
    for side, c in ((0, 0), (1, last)):
        other = aligned(side, z_got[side])
        own = edge[side]
        mixed = jnp.where(paired[side], (own + other) * 0.5, own)
        out_ref[:, span(c)] = jnp.where(own_valid[side] > 0.5, mixed - shift, 0.0)

    @pl.when(me != 0)
    def _():
        scatter_extra(devices - me).wait_send()

    @pl.when(me == 0)
    def _():
        @pl.loop(1, devices)
        def _(d):
            spread_extra(d).wait_send()

    @pl.when(me < owners)
    def _():
        @pl.loop(1, devices)
        def _(d):
            spread(d).wait_send()

    @pl.loop(1, devices)
    def _(d):
        @pl.when(lax.rem(me + d, devices) < owners)
        def _():
            scatter(d).wait_send()

def per_device(n_region, n_tile, quantized, block_scales, band_width, valid_count, prior_basis):
    tokens, feats = quantized.shape
    k = prior_basis.shape[1]
    devices = n_region * n_tile
    tiles = (k // 8) * (feats // 128)
    owners = min(devices, tiles)
    width = 128 * (tiles // owners)
    others = devices - 1
    dma = pltpu.SemaphoreType.DMA
    vmem = pl.BlockSpec(memory_space=pltpu.VMEM)
    smem = pl.BlockSpec(memory_space=pltpu.SMEM)
    projected, basis = pl.pallas_call(
        functools.partial(kernel, n_region, n_tile, owners, width),
        out_shape=(
            jax.ShapeDtypeStruct((k, tokens), F32),
            jax.ShapeDtypeStruct((k, feats), F32),
        ),
        in_specs=[smem, smem, pl.BlockSpec(memory_space=pltpu.HBM), vmem, vmem],
        out_specs=(vmem, vmem),
        scratch_shapes=[
            pltpu.VMEM((tokens, feats), BF16),
            pltpu.VMEM((2 * k + 16, feats), F32),
            pltpu.VMEM((2 * k, feats), BF16),
            pltpu.VMEM((2, k, BAND), F32),
            pltpu.VMEM((2, 2 * k + 32, BAND), BF16),
            pltpu.VMEM((2, 2 * k + 32, BAND), BF16),
            pltpu.VMEM((2, 2 * k, BAND), BF16),
            pltpu.VMEM((2, 2 * k, BAND), BF16),
            pltpu.VMEM((k, feats), F32),
            pltpu.VMEM((feats // 128, 256), F32),
            pltpu.VMEM((others, 8, width), F32),
            pltpu.VMEM((others, feats // 128, 256), F32),
            pltpu.VMEM((k, feats), F32),
            pltpu.VMEM((feats // 128, 256), F32),
            dma((tokens // BAND,)),
            dma((2,)), dma((2,)), dma((2,)), dma((2,)),
            dma((others,)), dma((others,)), dma(()), dma((others,)),
            dma((others,)), dma((others,)), dma((others,)), dma(()),
        ],
        compiler_params=pltpu.CompilerParams(
            collective_id=0, has_side_effects=True, vmem_limit_bytes=48 * 1024 * 1024
        ),
    )(band_width, valid_count, quantized, block_scales, prior_basis.T)
    return projected, basis.T


def solution(mesh):
    return jax.shard_map(
        functools.partial(per_device, mesh.shape["region"], mesh.shape["tile"]),
        mesh=mesh,
        in_specs=(
            P(("region", "tile"), None),
            P(None, ("region", "tile")),
            P(),
            P(("region", "tile")),
            P(),
        ),
        out_specs=(P(None, ("region", "tile")), P()),
        check_vma=False,
    )
```
